1024 devices in a mesh: brick: 64 (over x, y, core), node: 16 (over z).
Axes of the slice: x: 4, y: 8, z: 16, core: 2. Of those that a mesh axis runs over, the one named last changes fastest.
Arguments:
- density: float32 [64, 16, 2, 65536], P('brick', None, None, 'node'), may hold values from -68 to 68
- owner_map: int32 [64, 16], P('brick'), may hold values from 0 to 15, each once within a row
- view_rank: int32 [1024], replicated, may hold values from 0 to 1023, as said below
Outputs:
- image: float32 [4, 16, 4096], P(None, 'node', 'brick')
The draws below stay inside these ranges and needn't reach their ends.
Inputs may be any that keep to these rules, and one draw needn't show every extreme that they name: view_rank is a permutation: the rank of index i is i with its bit order reversed over the bits of 1023, XOR one drawn number.
All inputs are finite; a program needn't handle non-finite values.
Results may differ from the reference program's by a relative error of at most 0.0003.
Values sent between devices are 32-bit elements; how exact they have to be, the bound alone decides.
No kernel may reach another device: no remote copies, remote signals or barrier semaphores. Data moves between devices by JAX's collectives and lax.ppermute only.
A program may use at most 32 MiB of HBM per device.

```python
import math
import jax
import jax.numpy as jnp
from jax import lax

DEPTH = 2
PIX = 65536
RANKS = 1024
N_BRICK = 64
N_NODE = 16


def draw_view_rank(key, part):
    mixed = jax.random.fold_in(key, 11)
    flipper = jax.random.randint(mixed, (), 0, RANKS).astype(jnp.int32)
    levels = RANKS.bit_length() - 1
    index = jnp.arange(RANKS, dtype=jnp.int32)
    flipped = jnp.zeros((RANKS,), jnp.int32)
    for level in range(levels):
        flipped = flipped | (index >> level & 1) << levels - 1 - level
    return flipped ^ flipper


def draw_density(key, part):
    mixed = jax.random.fold_in(key, 23)
    key_cells, key_pixels, key_groups = jax.random.split(mixed, 3)
    shape = (N_BRICK, N_NODE, DEPTH, PIX)
    cells = jnp.clip(jax.random.normal(key_cells, shape, jnp.float32), -6.0, 6.0)
    pixel_scale = jnp.exp(jax.random.uniform(key_pixels, (PIX,), jnp.float32, math.log(0.25), math.log(8.0)))
    group_scale = jnp.exp(jax.random.uniform(key_groups, (N_BRICK, 1, 1, 1), jnp.float32, math.log(0.05), math.log(1.4)))
    return cells * group_scale * pixel_scale


def setup_inputs(seed: int = 0) -> dict:
    splits = jax.random.split(jax.random.key(seed), 4)
    density = draw_density(jax.random.fold_in(splits[3], 71), 0)
    owner_map = jax.vmap(lambda own: jax.random.permutation(own, N_NODE))(jax.random.split(splits[1], N_BRICK)).reshape((N_BRICK, N_NODE)).astype(jnp.int32)
    view_rank = draw_view_rank(jax.random.fold_in(splits[3], 71), 0)
    return dict(density=density, owner_map=owner_map, view_rank=view_rank)


def render(cells, kappa):
    shape = cells.shape[:-2] + cells.shape[-1:]
    red = jnp.zeros(shape, jnp.float32)
    green = jnp.zeros(shape, jnp.float32)
    blue = jnp.zeros(shape, jnp.float32)
    opacity = jnp.zeros(shape, jnp.float32)
    for slab in range(cells.shape[-2]):
        value = cells[..., slab, :]
        square = value * value
        alpha = 1.0 - jnp.exp(-kappa * square)
        weight = (1.0 - opacity) * alpha
        red = red + weight * jnp.exp(-0.125 * (value + 3.0) ** 2)
        green = green + weight * jnp.exp(-0.125 * square)
        blue = blue + weight * jnp.exp(-0.125 * (value - 3.0) ** 2)
        opacity = opacity + weight
    return jnp.stack([red, green, blue, opacity], axis=0)


def reference(density, owner_map, view_rank):
    kappa = 2.0 / (DEPTH * RANKS)
    inverse = jnp.argsort(owner_map, axis=1).astype(jnp.int32)
    order = jnp.argsort(view_rank).astype(jnp.int32)

    def step(total, device):
        group = device // N_NODE
        slot = device % N_NODE
        source = inverse[group, slot]
        picture = render(density[group, source], kappa)
        return total + (1.0 - total[3:4]) * picture, None

    start = jnp.zeros((4, PIX), jnp.float32)
    total, _ = lax.scan(step, start, order)
    return total.reshape(4, N_NODE, PIX // N_NODE)
```

```python
import functools
import jax
import jax.numpy as jnp
from jax import lax
from jax.experimental import pallas as pl
from jax.experimental.pallas import tpu as pltpu
from jax.sharding import PartitionSpec as P

LANES = 128
VMEM = pl.BlockSpec(memory_space=pltpu.VMEM)
SMEM = pl.BlockSpec(memory_space=pltpu.SMEM)


def over(front, back):
    keep = front[3]
    return tuple(front[k] + keep * back[k] for k in range(3)) + (keep * back[3],)


def pack_kernel(owner_ref, cells_ref, out_ref):
    bricks, depth, width = cells_ref.shape
    for brick in range(bricks):
        slot = owner_ref[0, brick]
        for slab in range(depth):
            for part in range(width // LANES):
                out_ref[part, pl.ds(slab * bricks + slot, 1), :] = cells_ref[brick, pl.ds(slab, 1), part * LANES:(part + 1) * LANES]


def pack(owner_map, cells):
    bricks, depth, width = cells.shape
    out = jax.ShapeDtypeStruct((width // LANES, depth * bricks, LANES), jnp.float32)
    return pl.pallas_call(pack_kernel, out_shape=out, in_specs=[SMEM, VMEM], out_specs=VMEM, name="pack", compiler_params=pltpu.CompilerParams(vmem_limit_bytes=4 << 20))(owner_map, cells)


def reverse(value, bits):
    return sum((value >> bit & 1) << (bits - 1 - bit) for bit in range(bits))


def composite_kernel(kappa, flip_ref, cells_ref, out_ref):
    chips, rows, lanes = cells_ref.shape
    nodes = out_ref.shape[1]
    depth = rows // nodes
    bits = chips.bit_length() - 1
    flip = flip_ref[0]
    swap = reverse(flip & (chips - 1), bits)
    red = jnp.zeros((nodes, lanes), jnp.float32)
    green = red
    blue = red
    keep = jnp.ones((nodes, lanes), jnp.float32)
    for rank in range(chips):
        chip = reverse(rank, bits) ^ swap
        for slab in range(depth):
            value = cells_ref[chip, slab * nodes:(slab + 1) * nodes, :]
            square = value * value
            alpha = 1.0 - jnp.exp(-kappa * square)
            weight = keep * alpha
            red = red + weight * jnp.exp(-0.125 * (value + 3.0) ** 2)
            green = green + weight * jnp.exp(-0.125 * square)
            blue = blue + weight * jnp.exp(-0.125 * (value - 3.0) ** 2)
            keep = keep - weight
    out_ref[0] = red
    out_ref[1] = green
    out_ref[2] = blue
    out_ref[3] = keep


def composite(cells, flip, nodes, kappa):
    out = jax.ShapeDtypeStruct((4, nodes, cells.shape[2]), jnp.float32)
    return pl.pallas_call(functools.partial(composite_kernel, kappa), out_shape=out, in_specs=[SMEM, VMEM], out_specs=VMEM, name="composite", compiler_params=pltpu.CompilerParams(vmem_limit_bytes=4 << 20))(flip, cells)


def finish_kernel(bits, flip_ref, side_ref, mine_ref, other_ref, out_ref):
    nodes, lanes = mine_ref.shape[1:]
    flip = flip_ref[0]
    side = side_ref[0]
    node_bits = nodes.bit_length() - 1
    mine = tuple(mine_ref[k] for k in range(4))
    other = tuple(other_ref[k] for k in range(4))
    first = (flip >> (bits - 1 - node_bits) & 1) == side
    front = tuple(jnp.where(first, a, b) for a, b in zip(mine, other))
    back = tuple(jnp.where(first, b, a) for a, b in zip(mine, other))
    total = over(front, back)
    row = lax.broadcasted_iota(jnp.int32, (nodes, lanes), 0)
    for bit in reversed(range(node_bits)):
        moved = tuple(pltpu.roll(a, 1 << bit, 0) for a in total) if 2 << bit == nodes else tuple(
            jnp.where((row >> bit & 1) == 0, pltpu.roll(a, nodes - (1 << bit), 0), pltpu.roll(a, 1 << bit, 0)) for a in total)
        ahead = (row >> bit & 1) == (flip >> (bits - 1 - bit) & 1)
        front = tuple(jnp.where(ahead, a, b) for a, b in zip(total, moved))
        back = tuple(jnp.where(ahead, b, a) for a, b in zip(total, moved))
        total = over(front, back)
    half = lanes // 2
    for k in range(4):
        line = total[k][:1] if k < 3 else 1.0 - total[k][:1]
        out_ref[k] = jnp.where(side == 0, line[:, :half], line[:, half:])


def finish(mine, other, flip, side, bits):
    out = jax.ShapeDtypeStruct((4, 1, mine.shape[2] // 2), jnp.float32)
    return pl.pallas_call(functools.partial(finish_kernel, bits), out_shape=out, in_specs=[SMEM, SMEM, VMEM, VMEM], out_specs=VMEM, name="finish", compiler_params=pltpu.CompilerParams(vmem_limit_bytes=4 << 20))(flip, side, mine, other)


def shards(density, owner_map, view_rank):
    nodes = lax.axis_size("node")
    bricks = lax.axis_size("brick")
    kappa = 2.0 / (density.shape[2] * bricks * nodes)
    bits = (bricks * nodes).bit_length() - 1
    same_core = [[2 * chip + core for chip in range(bricks // 2)] for core in range(2)]
    flip = view_rank[:1]
    side = (lax.axis_index("brick") & 1).reshape(1)
    packed = pack(owner_map, density[0])
    cells = lax.all_to_all(packed, "brick", 0, 0, axis_index_groups=same_core, tiled=True)
    mine = composite(cells, flip, nodes, kappa)
    other = lax.ppermute(mine, "brick", [(source, source ^ 1) for source in range(bricks)])
    return finish(mine, other, flip, side, bits)


def solution(mesh):
    in_specs = (P("brick", None, None, "node"), P("brick", None), P())
    out_specs = P(None, "node", "brick")
    return jax.shard_map(shards, mesh=mesh, in_specs=in_specs, out_specs=out_specs, check_vma=False)
```

```python
import functools
import math
import jax
import jax.numpy as jnp
from jax import lax
from jax.experimental import pallas as pl
from jax.experimental.pallas import tpu as pltpu
from jax.sharding import PartitionSpec as P

LANES = 128
VMEM = pl.BlockSpec(memory_space=pltpu.VMEM)
SMEM = pl.BlockSpec(memory_space=pltpu.SMEM)
HBM = pl.BlockSpec(memory_space=pltpu.HBM)
PARAMS = pltpu.CompilerParams(vmem_limit_bytes=4 << 20)


def over(front, back):
    keep = front[3]
    return tuple(front[k] + keep * back[k] for k in range(3)) + (keep * back[3],)


def pack_kernel(owner_hbm, cells_hbm, out_ref, owner_ref, owner_sem, sems):
    bricks = cells_hbm.shape[0]
    fetch = pltpu.make_async_copy(owner_hbm, owner_ref, owner_sem)
    fetch.start()
    fetch.wait()
    copies = [pltpu.make_async_copy(cells_hbm.at[brick], out_ref.at[:, owner_ref[0, brick]], sems.at[brick]) for brick in range(bricks)]
    for copy in copies:
        copy.start()
    for copy in copies:
        copy.wait()


def pack(owner_map, cells):
    bricks, depth, width = cells.shape
    parts = width // LANES
    tiles = cells.reshape(bricks, depth, parts, LANES).transpose(0, 2, 1, 3)
    return pl.pallas_call(
        pack_kernel,
        out_shape=pltpu.VMEM((parts, bricks, depth, LANES), jnp.float32),
        in_specs=[HBM, HBM],
        out_specs=VMEM,
        scratch_shapes=[pltpu.SMEM((1, bricks), jnp.int32), pltpu.SemaphoreType.DMA, pltpu.SemaphoreType.DMA((bricks,))],
        compiler_params=PARAMS,
        name="pack",
    )(pltpu.with_memory_space_constraint(owner_map, pltpu.HBM), pltpu.with_memory_space_constraint(tiles, pltpu.HBM))


def reverse(value, bits):
    return sum((value >> bit & 1) << (bits - 1 - bit) for bit in range(bits))


def composite_kernel(kappa, depth, flip_ref, cells_ref, out_ref):
    chips, rows, lanes = cells_ref.shape
    nodes = rows // depth
    bits = chips.bit_length() - 1
    swap = reverse(flip_ref[0] & (chips - 1), bits)
    scale = -0.125 * math.log2(math.e)
    red = jnp.zeros((nodes, lanes), jnp.float32)
    green = red
    blue = red
    keep = jnp.ones((nodes, lanes), jnp.float32)
    for rank in range(chips):
        chip = reverse(rank, bits) ^ swap
        for slab in range(depth):
            value = cells_ref[chip, pl.ds(slab, nodes, stride=depth), :]
            middle = value * value * scale
            slope = value * (6.0 * scale)
            side = middle + 9.0 * scale
            rest = keep * jnp.exp2(middle * (8.0 * kappa))
            weight = keep - rest
            red = red + weight * jnp.exp2(side + slope)
            green = green + weight * jnp.exp2(middle)
            blue = blue + weight * jnp.exp2(side - slope)
            keep = rest
    out_ref[0] = red
    out_ref[1] = green
    out_ref[2] = blue
    out_ref[3] = keep


def composite(cells, flip, kappa):
    chips, nodes, depth, lanes = cells.shape
    return pl.pallas_call(
        functools.partial(composite_kernel, kappa, depth),
        out_shape=pltpu.VMEM((4, nodes, lanes), jnp.float32),
        in_specs=[SMEM, VMEM],
        out_specs=VMEM,
        compiler_params=PARAMS,
        name="composite",
    )(flip, cells.reshape(chips, nodes * depth, lanes))


def finish_kernel(bits, flip_ref, side_ref, parts_ref, out_ref):
    nodes, lanes = parts_ref.shape[2:]
    flip = flip_ref[0]
    node_bits = nodes.bit_length() - 1
    ahead = flip >> (bits - 1 - node_bits) & 1
    total = over(tuple(parts_ref[ahead, k] for k in range(4)), tuple(parts_ref[1 - ahead, k] for k in range(4)))
    for bit in reversed(range(node_bits)):
        half = 1 << bit
        low = tuple(a[:half] for a in total)
        high = tuple(a[half:] for a in total)
        ahead = (flip >> (bits - 1 - bit) & 1) == 0
        front = tuple(jnp.where(ahead, a, b) for a, b in zip(low, high))
        back = tuple(jnp.where(ahead, b, a) for a, b in zip(low, high))
        total = over(front, back)
    first = side_ref[0] == 0
    for k in range(4):
        line = total[k] if k < 3 else 1.0 - total[k]
        out_ref[k] = jnp.where(first, line[:, :lanes // 2], line[:, lanes // 2:])


def finish(parts, flip, side, bits):
    out = pltpu.VMEM((4, 1, parts.shape[3] // 2), jnp.float32)
    return pl.pallas_call(functools.partial(finish_kernel, bits), out_shape=out, in_specs=[SMEM, SMEM, VMEM], out_specs=VMEM, compiler_params=PARAMS, name="finish")(flip, side, parts)


def shards(density, owner_map, view_rank):
    nodes = lax.axis_size("node")
    bricks = lax.axis_size("brick")
    kappa = 2.0 / (density.shape[2] * bricks * nodes)
    bits = (bricks * nodes).bit_length() - 1
    same_core = [[2 * chip + core for chip in range(bricks // 2)] for core in range(2)]
    same_chip = [[2 * chip, 2 * chip + 1] for chip in range(bricks // 2)]
    flip = view_rank[:1]
    side = (lax.axis_index("brick") & 1).reshape(1)
    packed = pack(owner_map, density[0])
    cells = lax.all_to_all(packed, "brick", 0, 0, axis_index_groups=same_core, tiled=True)
    mine = composite(cells, flip, kappa)
    both = lax.all_gather(mine, "brick", axis_index_groups=same_chip)
    return finish(both, flip, side, bits)


def solution(mesh):
    in_specs = (P("brick", None, None, "node"), P("brick", None), P())
    out_specs = P(None, "node", "brick")
    return jax.shard_map(shards, mesh=mesh, in_specs=in_specs, out_specs=out_specs, check_vma=False)
```

```python
import functools
import math
import jax
import jax.numpy as jnp
from jax import lax
from jax.experimental import pallas as pl
from jax.experimental.pallas import tpu as pltpu
from jax.sharding import PartitionSpec as P

LANES = 128
VMEM = pl.BlockSpec(memory_space=pltpu.VMEM)
HBM = pl.BlockSpec(memory_space=pltpu.HBM)
PARAMS = pltpu.CompilerParams(vmem_limit_bytes=4 << 20)


def over(front, back):
    keep = front[3]
    return tuple(front[k] + keep * back[k] for k in range(3)) + (keep * back[3],)


def pack_kernel(owner_hbm, ranks_hbm, cells_hbm, out_ref, ranks_ref, owner_ref, owner_sem, ranks_sem, sems):
    bricks = cells_hbm.shape[0]
    fetch = pltpu.make_async_copy(owner_hbm, owner_ref, owner_sem)
    fetch.start()
    ranks = pltpu.make_async_copy(ranks_hbm, ranks_ref, ranks_sem)
    ranks.start()
    fetch.wait()
    copies = [pltpu.make_async_copy(cells_hbm.at[brick], out_ref.at[:, owner_ref[0, brick]], sems.at[brick]) for brick in range(bricks)]
    for copy in copies:
        copy.start()
    for copy in copies:
        copy.wait()
    ranks.wait()


def on_hbm(value):
    return pltpu.with_memory_space_constraint(value, pltpu.HBM)


def pack(owner_map, view_rank, cells):
    bricks, depth, width = cells.shape
    parts = width // LANES
    tiles = cells.reshape(bricks, depth, parts, LANES).transpose(0, 2, 1, 3)
    return pl.pallas_call(
        pack_kernel,
        out_shape=(pltpu.VMEM((parts, bricks, depth, LANES), jnp.float32), pltpu.VMEM((view_rank.size // LANES, LANES), jnp.int32)),
        in_specs=[HBM, HBM, HBM],
        out_specs=(VMEM, VMEM),
        scratch_shapes=[pltpu.SMEM((1, bricks), jnp.int32), pltpu.SemaphoreType.DMA, pltpu.SemaphoreType.DMA, pltpu.SemaphoreType.DMA((bricks,))],
        compiler_params=PARAMS,
        name="pack",
    )(on_hbm(owner_map), on_hbm(view_rank.reshape(-1, LANES)), on_hbm(tiles))


def reverse(value, bits):
    return sum((value >> bit & 1) << (bits - 1 - bit) for bit in range(bits))


def composite_kernel(kappa, depth, ranks_ref, cells_ref, out_ref):
    chips, rows, lanes = cells_ref.shape
    nodes = rows // depth
    bits = chips.bit_length() - 1
    swap = reverse(ranks_ref[0, 0] & (chips - 1), bits)
    scale = -0.125 * math.log2(math.e)
    red = jnp.zeros((nodes, lanes), jnp.float32)
    green = red
    blue = red
    keep = jnp.ones((nodes, lanes), jnp.float32)
    for rank in range(chips):
        chip = reverse(rank, bits) ^ swap
        for slab in range(depth):
            value = cells_ref[chip, pl.ds(slab, nodes, stride=depth), :]
            middle = value * value * scale
            slope = value * (6.0 * scale)
            side = middle + 9.0 * scale
            rest = keep * jnp.exp2(middle * (8.0 * kappa))
            weight = keep - rest
            red = red + weight * jnp.exp2(side + slope)
            green = green + weight * jnp.exp2(middle)
            blue = blue + weight * jnp.exp2(side - slope)
            keep = rest
    out_ref[0] = red
    out_ref[1] = green
    out_ref[2] = blue
    out_ref[3] = keep


def composite(cells, ranks, kappa):
    chips, nodes, depth, lanes = cells.shape
    return pl.pallas_call(
        functools.partial(composite_kernel, kappa, depth),
        out_shape=pltpu.VMEM((4, nodes, lanes), jnp.float32),
        in_specs=[VMEM, VMEM],
        out_specs=VMEM,
        compiler_params=PARAMS,
        name="composite",
    )(ranks, cells.reshape(chips, nodes * depth, lanes))


def finish_kernel(bits, ranks_ref, parts_ref, out_ref):
    nodes, lanes = parts_ref.shape[2:]
    flip = ranks_ref[0, 0]
    node_bits = nodes.bit_length() - 1
    ahead = flip >> (bits - 1 - node_bits) & 1
    total = over(tuple(parts_ref[ahead, k] for k in range(4)), tuple(parts_ref[1 - ahead, k] for k in range(4)))
    for bit in reversed(range(node_bits)):
        half = 1 << bit
        low = tuple(a[:half] for a in total)
        high = tuple(a[half:] for a in total)
        ahead = (flip >> (bits - 1 - bit) & 1) == 0
        front = tuple(jnp.where(ahead, a, b) for a, b in zip(low, high))
        back = tuple(jnp.where(ahead, b, a) for a, b in zip(low, high))
        total = over(front, back)
    first = (lax.axis_index("brick") & 1) == 0
    for k in range(4):
        line = total[k] if k < 3 else 1.0 - total[k]
        out_ref[k] = jnp.where(first, line[:, :lanes // 2], line[:, lanes // 2:])


def finish(parts, ranks, bits):
    out = pltpu.VMEM((4, 1, parts.shape[3] // 2), jnp.float32)
    return pl.pallas_call(functools.partial(finish_kernel, bits), out_shape=out, in_specs=[VMEM, VMEM], out_specs=VMEM, compiler_params=PARAMS, name="finish")(ranks, parts)


def shards(density, owner_map, view_rank):
    nodes = lax.axis_size("node")
    bricks = lax.axis_size("brick")
    kappa = 2.0 / (density.shape[2] * bricks * nodes)
    bits = (bricks * nodes).bit_length() - 1
    same_core = [[2 * chip + core for chip in range(bricks // 2)] for core in range(2)]
    same_chip = [[2 * chip, 2 * chip + 1] for chip in range(bricks // 2)]
    packed, ranks = pack(owner_map, view_rank, density[0])
    cells = lax.all_to_all(packed, "brick", 0, 0, axis_index_groups=same_core, tiled=True)
    mine = composite(cells, ranks, kappa)
    both = lax.all_gather(mine, "brick", axis_index_groups=same_chip)
    return finish(both, ranks, bits)


def solution(mesh):
    in_specs = (P("brick", None, None, "node"), P("brick", None), P())
    out_specs = P(None, "node", "brick")
    return jax.shard_map(shards, mesh=mesh, in_specs=in_specs, out_specs=out_specs, check_vma=False)
```

```python
import functools
import math
import jax
import jax.numpy as jnp
from jax import lax
from jax.experimental import pallas as pl
from jax.experimental.pallas import tpu as pltpu
from jax.sharding import PartitionSpec as P

LANES = 128
ACROSS, ALONG = 4, 8


def chip_at(place):
    step, along = place // ALONG, place % ALONG
    return (step + along) % ACROSS * ALONG + along


def place_of(chip):
    return ((chip >> ALONG.bit_length() - 1) - chip & ACROSS - 1) * ALONG + (chip & ALONG - 1)


VMEM = pl.BlockSpec(memory_space=pltpu.VMEM)
HBM = pl.BlockSpec(memory_space=pltpu.HBM)
PARAMS = pltpu.CompilerParams(vmem_limit_bytes=4 << 20)


def over(front, back):
    keep = front[3]
    return tuple(front[k] + keep * back[k] for k in range(3)) + (keep * back[3],)


def pack_kernel(owner_hbm, ranks_hbm, cells_hbm, out_ref, ranks_ref, owner_ref, staged_ref, owner_sem, ranks_sem, sems):
    bricks = cells_hbm.shape[0]
    owner = pltpu.make_async_copy(owner_hbm, owner_ref, owner_sem)
    owner.start()
    copies = [pltpu.make_async_copy(cells_hbm.at[brick], staged_ref.at[brick], sems.at[brick]) for brick in range(bricks)]
    for copy in copies:
        copy.start()
    ranks = pltpu.make_async_copy(ranks_hbm, ranks_ref, ranks_sem)
    ranks.start()
    owner.wait()
    for brick in range(bricks):
        copies[brick].wait()
        slot = owner_ref[0, brick]
        for place in range(out_ref.shape[0]):
            out_ref[place, slot] = staged_ref[brick, chip_at(place)]
    ranks.wait()


def on_hbm(value):
    return pltpu.with_memory_space_constraint(value, pltpu.HBM)


def pack(owner_map, view_rank, cells):
    bricks, depth, width = cells.shape
    parts = width // LANES
    tiles = cells.reshape(bricks, depth, parts, LANES).transpose(0, 2, 1, 3)
    return pl.pallas_call(
        pack_kernel,
        out_shape=(pltpu.VMEM((parts, bricks, depth, LANES), jnp.float32), pltpu.VMEM((view_rank.size // LANES, LANES), jnp.int32)),
        in_specs=[HBM, HBM, HBM],
        out_specs=(VMEM, VMEM),
        scratch_shapes=[pltpu.SMEM((1, bricks), jnp.int32), pltpu.VMEM((bricks, parts, depth, LANES), jnp.float32), pltpu.SemaphoreType.DMA, pltpu.SemaphoreType.DMA, pltpu.SemaphoreType.DMA((bricks,))],
        compiler_params=PARAMS,
        name="pack",
    )(on_hbm(owner_map), on_hbm(view_rank.reshape(-1, LANES)), on_hbm(tiles))


def reverse(value, bits):
    return sum((value >> bit & 1) << (bits - 1 - bit) for bit in range(bits))


def composite_kernel(kappa, depth, ranks_ref, cells_ref, out_ref):
    chips, rows, lanes = cells_ref.shape
    nodes = rows // depth
    bits = chips.bit_length() - 1
    swap = reverse(ranks_ref[0, 0] & (chips - 1), bits)
    scale = -0.125 * math.log2(math.e)
    red = jnp.zeros((nodes, lanes), jnp.float32)
    green = red
    blue = red
    keep = jnp.ones((nodes, lanes), jnp.float32)
    for rank in range(chips):
        place = place_of(reverse(rank, bits) ^ swap)
        for slab in range(depth):
            value = cells_ref[place, pl.ds(slab, nodes, stride=depth), :]
            middle = value * value * scale
            slope = value * (6.0 * scale)
            side = middle + 9.0 * scale
            rest = keep * jnp.exp2(middle * (8.0 * kappa))
            weight = keep - rest
            red = red + weight * jnp.exp2(side + slope)
            green = green + weight * jnp.exp2(middle)
            blue = blue + weight * jnp.exp2(side - slope)
            keep = rest
    out_ref[0] = red
    out_ref[1] = green
    out_ref[2] = blue
    out_ref[3] = keep


def composite(cells, ranks, kappa):
    chips, nodes, depth, lanes = cells.shape
    return pl.pallas_call(
        functools.partial(composite_kernel, kappa, depth),
        out_shape=pltpu.VMEM((4, nodes, lanes), jnp.float32),
        in_specs=[VMEM, VMEM],
        out_specs=VMEM,
        compiler_params=PARAMS,
        name="composite",
    )(ranks, cells.reshape(chips, nodes * depth, lanes))


def finish_kernel(bits, ranks_ref, parts_ref, out_ref):
    nodes, lanes = parts_ref.shape[2:]
    flip = ranks_ref[0, 0]
    node_bits = nodes.bit_length() - 1
    ahead = flip >> (bits - 1 - node_bits) & 1
    total = over(tuple(parts_ref[ahead, k] for k in range(4)), tuple(parts_ref[1 - ahead, k] for k in range(4)))
    for bit in reversed(range(node_bits)):
        half = 1 << bit
        low = tuple(a[:half] for a in total)
        high = tuple(a[half:] for a in total)
        ahead = (flip >> (bits - 1 - bit) & 1) == 0
        front = tuple(jnp.where(ahead, a, b) for a, b in zip(low, high))
        back = tuple(jnp.where(ahead, b, a) for a, b in zip(low, high))
        total = over(front, back)
    first = (lax.axis_index("brick") & 1) == 0
    for k in range(4):
        line = total[k] if k < 3 else 1.0 - total[k]
        out_ref[k] = jnp.where(first, line[:, :lanes // 2], line[:, lanes // 2:])


def finish(parts, ranks, bits):
    out = pltpu.VMEM((4, 1, parts.shape[3] // 2), jnp.float32)
    return pl.pallas_call(functools.partial(finish_kernel, bits), out_shape=out, in_specs=[VMEM, VMEM], out_specs=VMEM, compiler_params=PARAMS, name="finish")(ranks, parts)


def shards(density, owner_map, view_rank):
    nodes = lax.axis_size("node")
    bricks = lax.axis_size("brick")
    kappa = 2.0 / (density.shape[2] * bricks * nodes)
    bits = (bricks * nodes).bit_length() - 1
    same_core = [[2 * chip + core for chip in map(chip_at, range(bricks // 2))] for core in range(2)]
    same_chip = [[2 * chip, 2 * chip + 1] for chip in range(bricks // 2)]
    packed, ranks = pack(owner_map, view_rank, density[0])
    cells = lax.all_to_all(packed, "brick", 0, 0, axis_index_groups=same_core, tiled=True)
    mine = composite(cells, ranks, kappa)
    both = lax.all_gather(mine, "brick", axis_index_groups=same_chip)
    return finish(both, ranks, bits)


def solution(mesh):
    in_specs = (P("brick", None, None, "node"), P("brick", None), P())
    out_specs = P(None, "node", "brick")
    return jax.shard_map(shards, mesh=mesh, in_specs=in_specs, out_specs=out_specs, check_vma=False)
```

```python
import functools
import math
import jax
import jax.numpy as jnp
from jax import lax
from jax.experimental import pallas as pl
from jax.experimental.pallas import tpu as pltpu
from jax.sharding import PartitionSpec as P

LANES = 128
ACROSS, ALONG = 4, 8


def chip_at(place):
    step, turn = place // ALONG, place % ALONG
    return (step + 1 + turn) % ACROSS * ALONG + -turn % ALONG


def place_of(chip):
    turn = -chip & ALONG - 1
    step = (chip >> ALONG.bit_length() - 1) - 1 - turn & ACROSS - 1
    return step * ALONG + turn


VMEM = pl.BlockSpec(memory_space=pltpu.VMEM)
HBM = pl.BlockSpec(memory_space=pltpu.HBM)
PARAMS = pltpu.CompilerParams(vmem_limit_bytes=4 << 20)


def over(front, back):
    keep = front[3]
    return tuple(front[k] + keep * back[k] for k in range(3)) + (keep * back[3],)


def pack_kernel(owner_hbm, ranks_hbm, cells_hbm, out_ref, ranks_ref, owner_ref, staged_ref, owner_sem, ranks_sem, sems):
    bricks = cells_hbm.shape[0]
    owner = pltpu.make_async_copy(owner_hbm, owner_ref, owner_sem)
    owner.start()
    copies = [pltpu.make_async_copy(cells_hbm.at[brick], staged_ref.at[brick], sems.at[brick]) for brick in range(bricks)]
    for copy in copies:
        copy.start()
    ranks = pltpu.make_async_copy(ranks_hbm, ranks_ref, ranks_sem)
    ranks.start()
    owner.wait()
    for brick in range(bricks):
        copies[brick].wait()
        slot = owner_ref[0, brick]
        for place in range(out_ref.shape[0]):
            out_ref[place, slot] = staged_ref[brick, chip_at(place)]
    ranks.wait()


def on_hbm(value):
    return pltpu.with_memory_space_constraint(value, pltpu.HBM)


def pack(owner_map, view_rank, cells):
    bricks, depth, width = cells.shape
    parts = width // LANES
    tiles = cells.reshape(bricks, depth, parts, LANES).transpose(0, 2, 1, 3)
    return pl.pallas_call(
        pack_kernel,
        out_shape=(pltpu.VMEM((parts, bricks, depth, LANES), jnp.float32), pltpu.VMEM((view_rank.size // LANES, LANES), jnp.int32)),
        in_specs=[HBM, HBM, HBM],
        out_specs=(VMEM, VMEM),
        scratch_shapes=[pltpu.SMEM((1, bricks), jnp.int32), pltpu.VMEM((bricks, parts, depth, LANES), jnp.float32), pltpu.SemaphoreType.DMA, pltpu.SemaphoreType.DMA, pltpu.SemaphoreType.DMA((bricks,))],
        compiler_params=PARAMS,
        name="pack",
    )(on_hbm(owner_map), on_hbm(view_rank.reshape(-1, LANES)), on_hbm(tiles))


def reverse(value, bits):
    return sum((value >> bit & 1) << (bits - 1 - bit) for bit in range(bits))


def composite_kernel(kappa, depth, ranks_ref, cells_ref, out_ref):
    chips, rows, lanes = cells_ref.shape
    nodes = rows // depth
    bits = chips.bit_length() - 1
    swap = reverse(ranks_ref[0, 0] & (chips - 1), bits)
    scale = -0.125 * math.log2(math.e)
    red = jnp.zeros((nodes, lanes), jnp.float32)
    green = red
    blue = red
    keep = jnp.ones((nodes, lanes), jnp.float32)
    for rank in range(chips):
        place = place_of(reverse(rank, bits) ^ swap)
        for slab in range(depth):
            value = cells_ref[place, pl.ds(slab, nodes, stride=depth), :]
            middle = value * value * scale
            slope = value * (6.0 * scale)
            side = middle + 9.0 * scale
            rest = keep * jnp.exp2(middle * (8.0 * kappa))
            weight = keep - rest
            red = red + weight * jnp.exp2(side + slope)
            green = green + weight * jnp.exp2(middle)
            blue = blue + weight * jnp.exp2(side - slope)
            keep = rest
    out_ref[0] = red
    out_ref[1] = green
    out_ref[2] = blue
    out_ref[3] = keep


def composite(cells, ranks, kappa):
    chips, nodes, depth, lanes = cells.shape
    return pl.pallas_call(
        functools.partial(composite_kernel, kappa, depth),
        out_shape=pltpu.VMEM((4, nodes, lanes), jnp.float32),
        in_specs=[VMEM, VMEM],
        out_specs=VMEM,
        compiler_params=PARAMS,
        name="composite",
    )(ranks, cells.reshape(chips, nodes * depth, lanes))


def finish_kernel(bits, ranks_ref, parts_ref, out_ref):
    nodes, lanes = parts_ref.shape[2:]
    flip = ranks_ref[0, 0]
    node_bits = nodes.bit_length() - 1
    ahead = flip >> (bits - 1 - node_bits) & 1
    total = over(tuple(parts_ref[ahead, k] for k in range(4)), tuple(parts_ref[1 - ahead, k] for k in range(4)))
    for bit in reversed(range(node_bits)):
        half = 1 << bit
        low = tuple(a[:half] for a in total)
        high = tuple(a[half:] for a in total)
        ahead = (flip >> (bits - 1 - bit) & 1) == 0
        front = tuple(jnp.where(ahead, a, b) for a, b in zip(low, high))
        back = tuple(jnp.where(ahead, b, a) for a, b in zip(low, high))
        total = over(front, back)
    first = (lax.axis_index("brick") & 1) == 0
    for k in range(4):
        line = total[k] if k < 3 else 1.0 - total[k]
        out_ref[k] = jnp.where(first, line[:, :lanes // 2], line[:, lanes // 2:])


def finish(parts, ranks, bits):
    out = pltpu.VMEM((4, 1, parts.shape[3] // 2), jnp.float32)
    return pl.pallas_call(functools.partial(finish_kernel, bits), out_shape=out, in_specs=[VMEM, VMEM], out_specs=VMEM, compiler_params=PARAMS, name="finish")(ranks, parts)


def shards(density, owner_map, view_rank):
    nodes = lax.axis_size("node")
    bricks = lax.axis_size("brick")
    kappa = 2.0 / (density.shape[2] * bricks * nodes)
    bits = (bricks * nodes).bit_length() - 1
    same_core = [[2 * chip + core for chip in map(chip_at, range(bricks // 2))] for core in range(2)]
    same_chip = [[2 * chip, 2 * chip + 1] for chip in range(bricks // 2)]
    packed, ranks = pack(owner_map, view_rank, density[0])
    cells = lax.all_to_all(packed, "brick", 0, 0, axis_index_groups=same_core, tiled=True)
    mine = composite(cells, ranks, kappa)
    both = lax.all_gather(mine, "brick", axis_index_groups=same_chip)
    return finish(both, ranks, bits)


def solution(mesh):
    in_specs = (P("brick", None, None, "node"), P("brick", None), P())
    out_specs = P(None, "node", "brick")
    return jax.shard_map(shards, mesh=mesh, in_specs=in_specs, out_specs=out_specs, check_vma=False)
```

```python
import functools
import math
import jax
import jax.numpy as jnp
from jax import lax
from jax.experimental import pallas as pl
from jax.experimental.pallas import tpu as pltpu
from jax.sharding import PartitionSpec as P

LANES = 128
ACROSS, ALONG = 4, 8


SHIFTS = (1, 0, 3, 0, 1, 2, 0, 1)
TABLE = sum(shift << 2 * turn for turn, shift in enumerate(SHIFTS))


def chip_at(place):
    step, turn = place // ALONG, place % ALONG
    return (step + SHIFTS[turn]) % ACROSS * ALONG + -turn % ALONG


def place_of(chip):
    turn = -chip & ALONG - 1
    shift = jnp.int32(TABLE) >> 2 * turn
    step = (chip >> ALONG.bit_length() - 1) - shift & ACROSS - 1
    return step * ALONG + turn


VMEM = pl.BlockSpec(memory_space=pltpu.VMEM)
HBM = pl.BlockSpec(memory_space=pltpu.HBM)
PARAMS = pltpu.CompilerParams(vmem_limit_bytes=4 << 20)


def over(front, back):
    keep = front[3]
    return tuple(front[k] + keep * back[k] for k in range(3)) + (keep * back[3],)


def pack_kernel(owner_hbm, ranks_hbm, cells_hbm, out_ref, ranks_ref, owner_ref, staged_ref, owner_sem, ranks_sem, sems):
    bricks = cells_hbm.shape[0]
    owner = pltpu.make_async_copy(owner_hbm, owner_ref, owner_sem)
    owner.start()
    copies = [pltpu.make_async_copy(cells_hbm.at[brick], staged_ref.at[brick], sems.at[brick]) for brick in range(bricks)]
    for copy in copies:
        copy.start()
    ranks = pltpu.make_async_copy(ranks_hbm, ranks_ref, ranks_sem)
    ranks.start()
    owner.wait()
    for brick in range(bricks):
        copies[brick].wait()
        slot = owner_ref[0, brick]
        for place in range(out_ref.shape[0]):
            out_ref[place, slot] = staged_ref[brick, chip_at(place)]
    ranks.wait()


def on_hbm(value):
    return pltpu.with_memory_space_constraint(value, pltpu.HBM)


def pack(owner_map, view_rank, cells):
    bricks, depth, width = cells.shape
    parts = width // LANES
    tiles = cells.reshape(bricks, depth, parts, LANES).transpose(0, 2, 1, 3)
    return pl.pallas_call(
        pack_kernel,
        out_shape=(pltpu.VMEM((parts, bricks, depth, LANES), jnp.float32), pltpu.VMEM((view_rank.size // LANES, LANES), jnp.int32)),
        in_specs=[HBM, HBM, HBM],
        out_specs=(VMEM, VMEM),
        scratch_shapes=[pltpu.SMEM((1, bricks), jnp.int32), pltpu.VMEM((bricks, parts, depth, LANES), jnp.float32), pltpu.SemaphoreType.DMA, pltpu.SemaphoreType.DMA, pltpu.SemaphoreType.DMA((bricks,))],
        compiler_params=PARAMS,
        name="pack",
    )(on_hbm(owner_map), on_hbm(view_rank.reshape(-1, LANES)), on_hbm(tiles))


def reverse(value, bits):
    return sum((value >> bit & 1) << (bits - 1 - bit) for bit in range(bits))


def composite_kernel(kappa, depth, ranks_ref, cells_ref, out_ref):
    chips, rows, lanes = cells_ref.shape
    nodes = rows // depth
    bits = chips.bit_length() - 1
    swap = reverse(ranks_ref[0, 0] & (chips - 1), bits)
    scale = -0.125 * math.log2(math.e)
    red = jnp.zeros((nodes, lanes), jnp.float32)
    green = red
    blue = red
    keep = jnp.ones((nodes, lanes), jnp.float32)
    for rank in range(chips):
        place = place_of(reverse(rank, bits) ^ swap)
        for slab in range(depth):
            value = cells_ref[place, pl.ds(slab, nodes, stride=depth), :]
            middle = value * value * scale
            slope = value * (6.0 * scale)
            side = middle + 9.0 * scale
            rest = keep * jnp.exp2(middle * (8.0 * kappa))
            weight = keep - rest
            red = red + weight * jnp.exp2(side + slope)
            green = green + weight * jnp.exp2(middle)
            blue = blue + weight * jnp.exp2(side - slope)
            keep = rest
    out_ref[0] = red
    out_ref[1] = green
    out_ref[2] = blue
    out_ref[3] = keep


def composite(cells, ranks, kappa):
    chips, nodes, depth, lanes = cells.shape
    return pl.pallas_call(
        functools.partial(composite_kernel, kappa, depth),
        out_shape=pltpu.VMEM((4, nodes, lanes), jnp.float32),
        in_specs=[VMEM, VMEM],
        out_specs=VMEM,
        compiler_params=PARAMS,
        name="composite",
    )(ranks, cells.reshape(chips, nodes * depth, lanes))


def finish_kernel(bits, ranks_ref, parts_ref, out_ref):
    nodes, lanes = parts_ref.shape[2:]
    flip = ranks_ref[0, 0]
    node_bits = nodes.bit_length() - 1
    ahead = flip >> (bits - 1 - node_bits) & 1
    total = over(tuple(parts_ref[ahead, k] for k in range(4)), tuple(parts_ref[1 - ahead, k] for k in range(4)))
    for bit in reversed(range(node_bits)):
        half = 1 << bit
        low = tuple(a[:half] for a in total)
        high = tuple(a[half:] for a in total)
        ahead = (flip >> (bits - 1 - bit) & 1) == 0
        front = tuple(jnp.where(ahead, a, b) for a, b in zip(low, high))
        back = tuple(jnp.where(ahead, b, a) for a, b in zip(low, high))
        total = over(front, back)
    first = (lax.axis_index("brick") & 1) == 0
    for k in range(4):
        line = total[k] if k < 3 else 1.0 - total[k]
        out_ref[k] = jnp.where(first, line[:, :lanes // 2], line[:, lanes // 2:])


def finish(parts, ranks, bits):
    out = pltpu.VMEM((4, 1, parts.shape[3] // 2), jnp.float32)
    return pl.pallas_call(functools.partial(finish_kernel, bits), out_shape=out, in_specs=[VMEM, VMEM], out_specs=VMEM, compiler_params=PARAMS, name="finish")(ranks, parts)


def shards(density, owner_map, view_rank):
    nodes = lax.axis_size("node")
    bricks = lax.axis_size("brick")
    kappa = 2.0 / (density.shape[2] * bricks * nodes)
    bits = (bricks * nodes).bit_length() - 1
    same_core = [[2 * chip + core for chip in map(chip_at, range(bricks // 2))] for core in range(2)]
    same_chip = [[2 * chip, 2 * chip + 1] for chip in range(bricks // 2)]
    packed, ranks = pack(owner_map, view_rank, density[0])
    cells = lax.all_to_all(packed, "brick", 0, 0, axis_index_groups=same_core, tiled=True)
    mine = composite(cells, ranks, kappa)
    both = lax.all_gather(mine, "brick", axis_index_groups=same_chip)
    return finish(both, ranks, bits)


def solution(mesh):
    in_specs = (P("brick", None, None, "node"), P("brick", None), P())
    out_specs = P(None, "node", "brick")
    return jax.shard_map(shards, mesh=mesh, in_specs=in_specs, out_specs=out_specs, check_vma=False)
```

```python
import functools
import math
import jax
import jax.numpy as jnp
from jax import lax
from jax.experimental import pallas as pl
from jax.experimental.pallas import tpu as pltpu
from jax.sharding import PartitionSpec as P

LANES = 128
ACROSS, ALONG = 4, 8


SHIFTS = (1, 1, 3, 0, 1, 3, 0, 1)
TABLE = sum(shift << 2 * turn for turn, shift in enumerate(SHIFTS))


def chip_at(place):
    step, turn = place // ALONG, place % ALONG
    return (step + SHIFTS[turn]) % ACROSS * ALONG + -turn % ALONG


def place_of(chip):
    turn = -chip & ALONG - 1
    shift = jnp.int32(TABLE) >> 2 * turn
    step = (chip >> ALONG.bit_length() - 1) - shift & ACROSS - 1
    return step * ALONG + turn


VMEM = pl.BlockSpec(memory_space=pltpu.VMEM)
HBM = pl.BlockSpec(memory_space=pltpu.HBM)
PARAMS = pltpu.CompilerParams(vmem_limit_bytes=4 << 20)


def over(front, back):
    keep = front[3]
    return tuple(front[k] + keep * back[k] for k in range(3)) + (keep * back[3],)


def pack_kernel(owner_hbm, ranks_hbm, cells_hbm, out_ref, ranks_ref, owner_ref, staged_ref, owner_sem, ranks_sem, sems):
    bricks = cells_hbm.shape[0]
    owner = pltpu.make_async_copy(owner_hbm, owner_ref, owner_sem)
    owner.start()
    copies = [pltpu.make_async_copy(cells_hbm.at[brick], staged_ref.at[brick], sems.at[brick]) for brick in range(bricks)]
    for copy in copies:
        copy.start()
    ranks = pltpu.make_async_copy(ranks_hbm, ranks_ref, ranks_sem)
    ranks.start()
    owner.wait()
    for brick in range(bricks):
        copies[brick].wait()
        slot = owner_ref[0, brick]
        for place in range(out_ref.shape[0]):
            out_ref[place, slot] = staged_ref[brick, chip_at(place)]
    ranks.wait()


def on_hbm(value):
    return pltpu.with_memory_space_constraint(value, pltpu.HBM)


def pack(owner_map, view_rank, cells):
    bricks, depth, width = cells.shape
    parts = width // LANES
    tiles = cells.reshape(bricks, depth, parts, LANES).transpose(0, 2, 1, 3)
    return pl.pallas_call(
        pack_kernel,
        out_shape=(pltpu.VMEM((parts, bricks, depth, LANES), jnp.float32), pltpu.VMEM((view_rank.size // LANES, LANES), jnp.int32)),
        in_specs=[HBM, HBM, HBM],
        out_specs=(VMEM, VMEM),
        scratch_shapes=[pltpu.SMEM((1, bricks), jnp.int32), pltpu.VMEM((bricks, parts, depth, LANES), jnp.float32), pltpu.SemaphoreType.DMA, pltpu.SemaphoreType.DMA, pltpu.SemaphoreType.DMA((bricks,))],
        compiler_params=PARAMS,
        name="pack",
    )(on_hbm(owner_map), on_hbm(view_rank.reshape(-1, LANES)), on_hbm(tiles))


def reverse(value, bits):
    return sum((value >> bit & 1) << (bits - 1 - bit) for bit in range(bits))


def composite_kernel(kappa, depth, ranks_ref, cells_ref, out_ref):
    chips, rows, lanes = cells_ref.shape
    nodes = rows // depth
    bits = chips.bit_length() - 1
    swap = reverse(ranks_ref[0, 0] & (chips - 1), bits)
    scale = -0.125 * math.log2(math.e)
    red = jnp.zeros((nodes, lanes), jnp.float32)
    green = red
    blue = red
    keep = jnp.ones((nodes, lanes), jnp.float32)
    for rank in range(chips):
        place = place_of(reverse(rank, bits) ^ swap)
        for slab in range(depth):
            value = cells_ref[place, pl.ds(slab, nodes, stride=depth), :]
            middle = value * value * scale
            slope = value * (6.0 * scale)
            side = middle + 9.0 * scale
            rest = keep * jnp.exp2(middle * (8.0 * kappa))
            weight = keep - rest
            red = red + weight * jnp.exp2(side + slope)
            green = green + weight * jnp.exp2(middle)
            blue = blue + weight * jnp.exp2(side - slope)
            keep = rest
    out_ref[0] = red
    out_ref[1] = green
    out_ref[2] = blue
    out_ref[3] = keep


def composite(cells, ranks, kappa):
    chips, nodes, depth, lanes = cells.shape
    return pl.pallas_call(
        functools.partial(composite_kernel, kappa, depth),
        out_shape=pltpu.VMEM((4, nodes, lanes), jnp.float32),
        in_specs=[VMEM, VMEM],
        out_specs=VMEM,
        compiler_params=PARAMS,
        name="composite",
    )(ranks, cells.reshape(chips, nodes * depth, lanes))


def finish_kernel(bits, ranks_ref, parts_ref, out_ref):
    nodes, lanes = parts_ref.shape[2:]
    flip = ranks_ref[0, 0]
    node_bits = nodes.bit_length() - 1
    ahead = flip >> (bits - 1 - node_bits) & 1
    total = over(tuple(parts_ref[ahead, k] for k in range(4)), tuple(parts_ref[1 - ahead, k] for k in range(4)))
    for bit in reversed(range(node_bits)):
        half = 1 << bit
        low = tuple(a[:half] for a in total)
        high = tuple(a[half:] for a in total)
        ahead = (flip >> (bits - 1 - bit) & 1) == 0
        front = tuple(jnp.where(ahead, a, b) for a, b in zip(low, high))
        back = tuple(jnp.where(ahead, b, a) for a, b in zip(low, high))
        total = over(front, back)
    first = (lax.axis_index("brick") & 1) == 0
    for k in range(4):
        line = total[k] if k < 3 else 1.0 - total[k]
        out_ref[k] = jnp.where(first, line[:, :lanes // 2], line[:, lanes // 2:])


def finish(parts, ranks, bits):
    out = pltpu.VMEM((4, 1, parts.shape[3] // 2), jnp.float32)
    return pl.pallas_call(functools.partial(finish_kernel, bits), out_shape=out, in_specs=[VMEM, VMEM], out_specs=VMEM, compiler_params=PARAMS, name="finish")(ranks, parts)


def shards(density, owner_map, view_rank):
    nodes = lax.axis_size("node")
    bricks = lax.axis_size("brick")
    kappa = 2.0 / (density.shape[2] * bricks * nodes)
    bits = (bricks * nodes).bit_length() - 1
    same_core = [[2 * chip + core for chip in map(chip_at, range(bricks // 2))] for core in range(2)]
    same_chip = [[2 * chip, 2 * chip + 1] for chip in range(bricks // 2)]
    packed, ranks = pack(owner_map, view_rank, density[0])
    cells = lax.all_to_all(packed, "brick", 0, 0, axis_index_groups=same_core, tiled=True)
    mine = composite(cells, ranks, kappa)
    both = lax.all_gather(mine, "brick", axis_index_groups=same_chip)
    return finish(both, ranks, bits)


def solution(mesh):
    in_specs = (P("brick", None, None, "node"), P("brick", None), P())
    out_specs = P(None, "node", "brick")
    return jax.shard_map(shards, mesh=mesh, in_specs=in_specs, out_specs=out_specs, check_vma=False)
```
